32 devices in a mesh: group: 1, seq: 32 (over z, y, x, core).
Axes of the slice: x: 2, y: 2, z: 4, core: 2. Of those that a mesh axis runs over, the one named last changes fastest.
Arguments:
- enc_x: bfloat16 [256, 1280], P(('group', 'seq')), may hold values from -1.5 to 1.5
- enc_qkv: bfloat16 [256, 3, 640], P(('group', 'seq'))
- w_eo: bfloat16 [640, 1280], replicated, may hold values from -0.25 to 0.25
- w_kv: bfloat16 [1280, 2048], replicated, may hold values from -0.15625 to 0.15625
- dec_x: bfloat16 [32, 8192], P(('group', 'seq')), may hold values from -1.5 to 1.5
- w_q: bfloat16 [8192, 8192], P(None, 'seq'), may hold values from -0.0625 to 0.0625
- w_o: bfloat16 [8192, 8192], P(None, 'seq'), may hold values from -0.0625 to 0.0625
- cache_kv: bfloat16 [32, 4, 128, 2048], P(('group', 'seq'))
- doc_tile: int32 [32], P(('group', 'seq')), may hold values from 0 to 1
- cached_count: int32 [32], P(('group', 'seq')), may hold values from 0 to 3
Outputs:
- dec_out: bfloat16 [32, 8192], P(('group', 'seq'))
The draws below stay inside these ranges and needn't reach their ends.
All inputs are finite; a program needn't handle non-finite values.
Results may differ from the reference program's by a relative error of at most 0.017.
The reference program's roundings to bfloat16 on the way count: a program that leaves them out, or rounds other values in their place, can miss the bound.
Values may be sent and summed in bfloat16 or wider, within the bound.
A program may use at most 64 MiB of HBM per device.

```python
import jax
import jax.numpy as jnp
from jax import lax

EW = 1280
EH = 8
EHD = 80
D = 8192
HD = 128
TILE_LEN = 128
SLOTS = 4
EA = 640
KVW = 1024
ETOK = 256
NEW_TILES = 2
DOCS = 32


def draw_enc_qkv(key, part):
    first = jax.random.fold_in(jax.random.fold_in(key, 11), 0)
    base = jax.random.normal(first, (ETOK, 3, EA), jnp.float32)
    which = jnp.arange(3).reshape(1, 3, 1) == 0
    scale = jnp.full((ETOK, 1, 1), 1.8, jnp.float32)
    base = base * jnp.where(which, scale, 1.0)
    return base.astype(jnp.bfloat16)


def draw_cache_kv(key, part):
    first = jax.random.fold_in(jax.random.fold_in(key, 23), 0)
    base = jax.random.normal(first, (DOCS, SLOTS, TILE_LEN, 2 * KVW), jnp.float32)
    return base.astype(jnp.bfloat16)


def with_ends(entries, own_key, least, top_value):
    spot = [jax.random.randint(jax.random.fold_in(own_key, axis), (), 0, length) for axis, length in enumerate(entries.shape)]
    longest = entries.shape.index(max(entries.shape))
    beside = spot[:longest] + [(spot[longest] + 1) % entries.shape[longest]] + spot[longest + 1:]
    return entries.at[tuple(spot)].set(least).at[tuple(beside)].set(top_value)


def level_of(key, dims, shards, smallest, top_value):
    loudness, own = 1.0, jax.random.fold_in(key, 6)
    for dim, parts in shards:
        heights = jnp.exp(jax.random.uniform(jax.random.fold_in(own, dim), (parts,), jnp.float32, smallest / len(shards), top_value / len(shards)))
        loudness = loudness * jnp.repeat(heights, dims[dim] // parts).reshape([-1 if axis == dim else 1 for axis in range(len(dims))])
    return loudness


def gaussian(own_key, dims, deviation, limit, cuts=(), kind=jnp.bfloat16):
    factor_of = level_of(own_key, dims, cuts, -0.22, 0.18) if cuts else 1.0
    drawn = jax.random.normal(own_key, dims, jnp.float32) * deviation * factor_of
    return jnp.minimum(jnp.maximum(drawn, -limit), limit).astype(kind)


def setup_inputs(seed: int = 0, part: int = 0) -> dict:
    seeds = jax.random.split(jax.random.key(seed), 11)
    part_keys = jax.random.split(jax.random.fold_in(seeds[10], part), 11)
    return {
        "enc_x": gaussian(part_keys[0], (ETOK, EW), 0.1, 1.5, ((0, 32),)),
        "enc_qkv": draw_enc_qkv(jax.random.fold_in(jax.random.fold_in(seeds[10], part), 71), part),
        "w_eo": gaussian(seeds[2], (EA, EW), EA ** -0.5, 0.25),
        "w_kv": gaussian(seeds[3], (EW, 2 * KVW), EW ** -0.5, 0.15625),
        "dec_x": gaussian(part_keys[4], (DOCS, D), 0.1, 1.5, ((0, 32),)),
        "w_q": gaussian(seeds[5], (D, D), D ** -0.5, 0.0625, ((1, 32),)),
        "w_o": gaussian(seeds[6], (D, D), D ** -0.5, 0.0625, ((1, 32),)),
        "cache_kv": draw_cache_kv(jax.random.fold_in(jax.random.fold_in(seeds[10], part), 71), part),
        "doc_tile": with_ends(jax.random.randint(part_keys[8], (DOCS,), 0, NEW_TILES), jax.random.fold_in(part_keys[8], 1), 0, NEW_TILES - 1).astype(jnp.int32),
        "cached_count": with_ends(jax.random.randint(part_keys[9], (DOCS,), 0, SLOTS), jax.random.fold_in(part_keys[9], 1), 0, SLOTS - 1).astype(jnp.int32),
    }


def layer_norm(values):
    center = values - lax.optimization_barrier(jnp.mean(values, axis=-1, keepdims=True))
    spread = lax.optimization_barrier(jnp.mean(center * center, axis=-1, keepdims=True))
    return center * lax.rsqrt(spread + 1e-05)

def doc_attend(query_row, doc_kv, filled):
    length = doc_kv.shape[0]
    width = doc_kv.shape[1] // 2
    kv_heads = width // HD
    query_heads = query_row.astype(jnp.float32).reshape(kv_heads, -1, HD)
    key_heads = doc_kv[:, :width].astype(jnp.float32).reshape(length, kv_heads, HD)
    value_heads = doc_kv[:, width:].astype(jnp.float32).reshape(length, kv_heads, HD)
    scores = jnp.einsum('gqd,kgd->gqk', query_heads, key_heads, precision=lax.Precision.HIGHEST) * HD ** (-0.5)
    inside = jnp.arange(length, dtype=jnp.int32) // TILE_LEN <= filled
    scores = jnp.where(inside[None, None, :], scores, -jnp.inf)
    weights = jax.nn.softmax(scores, axis=-1).astype(jnp.bfloat16).astype(jnp.float32)
    result = jnp.einsum('gqk,kgd->gqd', weights, value_heads, precision=lax.Precision.HIGHEST)
    return result.reshape(-1).astype(jnp.bfloat16)

def reference(enc_x, enc_qkv, w_eo, w_kv, dec_x, w_q, w_o, cache_kv, doc_tile, cached_count):
    query_all = enc_qkv[:, 0].reshape(ETOK, EH, EHD).transpose(1, 0, 2)
    key_all = enc_qkv[:, 1].reshape(ETOK, EH, EHD).transpose(1, 0, 2)
    value_all = enc_qkv[:, 2].reshape(ETOK, EH, EHD).transpose(1, 0, 2)

    def one_head(triple):
        query_head, key_head, value_head = triple
        scores = jnp.dot(query_head, key_head.T, preferred_element_type=jnp.float32) * EHD ** (-0.5)
        weights = jax.nn.softmax(scores, axis=-1).astype(jnp.bfloat16)
        return jnp.dot(weights, value_head, preferred_element_type=jnp.float32)
    heads_out = lax.map(one_head, (query_all, key_all, value_all))
    enc_attn = heads_out.transpose(1, 0, 2).reshape(ETOK, EA).astype(jnp.bfloat16)
    resid = enc_x.astype(jnp.float32) + jnp.dot(enc_attn, w_eo, preferred_element_type=jnp.float32)
    features = layer_norm(resid).astype(jnp.bfloat16)
    new_kv = jnp.dot(features, w_kv, preferred_element_type=jnp.float32).astype(jnp.bfloat16)
    tiles = new_kv.reshape(NEW_TILES, TILE_LEN, 2 * KVW)
    x_float = dec_x.astype(jnp.float32)
    normed = (x_float * lax.rsqrt(lax.optimization_barrier(jnp.mean(x_float * x_float, axis=-1, keepdims=True)) + 1e-05)).astype(jnp.bfloat16)
    queries = jnp.dot(normed, w_q, preferred_element_type=jnp.float32).astype(jnp.bfloat16)

    def one_doc(quad):
        query_row, cache_doc, tile_id, filled = quad
        chosen = lax.dynamic_index_in_dim(tiles, tile_id.astype(jnp.int32), 0, keepdims=True)
        zero = jnp.zeros((), jnp.int32)
        doc_kv = lax.dynamic_update_slice(cache_doc, chosen, (filled.astype(jnp.int32), zero, zero))
        return doc_attend(query_row, doc_kv.reshape(SLOTS * TILE_LEN, 2 * KVW), filled)
    dec_attn = lax.map(one_doc, (queries, cache_kv, doc_tile, cached_count))
    attn_out = jnp.dot(dec_attn, w_o, preferred_element_type=jnp.float32).astype(jnp.bfloat16)
    return (x_float + attn_out.astype(jnp.float32)).astype(jnp.bfloat16)
```

```python
import functools

import jax
import jax.numpy as jnp
from jax import lax
from jax.experimental import pallas as pl
from jax.experimental.pallas import tpu as pltpu
from jax.sharding import PartitionSpec as P

EH = 8
EHD = 80
HD = 128
TILE_LEN = 128
MESH = pl.DeviceIdType.MESH


def layer_norm(values):
    center = values - jnp.mean(values, axis=-1, keepdims=True)
    spread = jnp.mean(center * center, axis=-1, keepdims=True)
    return center * lax.rsqrt(spread + 1e-05)


def doc_attend(query_row, doc_kv, filled):
    length = doc_kv.shape[0]
    width = doc_kv.shape[1] // 2
    kv_heads = width // HD
    query_heads = query_row.reshape(kv_heads, -1, HD)
    key_heads = doc_kv[:, :width].reshape(length, kv_heads, HD)
    value_heads = doc_kv[:, width:].reshape(length, kv_heads, HD)
    scores = jnp.einsum(
        "gqd,kgd->gqk", query_heads, key_heads, preferred_element_type=jnp.float32
    ) * HD ** (-0.5)
    inside = jnp.arange(length, dtype=jnp.int32) // TILE_LEN <= filled
    scores = jnp.where(inside[None, None, :], scores, -jnp.inf)
    weights = jax.nn.softmax(scores, axis=-1).astype(jnp.bfloat16)
    result = jnp.einsum("gqk,kgd->gqd", weights, value_heads, preferred_element_type=jnp.float32)
    return result.reshape(1, -1).astype(jnp.bfloat16)


def local(enc_x, enc_qkv, w_eo, w_kv, dec_x, w_q, w_o, cache_kv, doc_tile, cached_count):
    tok_rows = enc_x.shape[0]
    query_heads = enc_qkv[:, 0].reshape(tok_rows, EH, EHD)
    key_piece = lax.all_gather(enc_qkv[:, 1], "seq", axis=0, tiled=True)
    value_piece = lax.all_gather(enc_qkv[:, 2], "seq", axis=0, tiled=True)
    length = key_piece.shape[0]
    key_heads = key_piece.reshape(length, EH, EHD)
    value_heads = value_piece.reshape(length, EH, EHD)
    scores = jnp.einsum(
        "qhd,khd->hqk", query_heads, key_heads, preferred_element_type=jnp.float32
    ) * EHD ** (-0.5)
    old_max = jnp.full((EH, tok_rows), -1e30, jnp.float32)
    new_max = jnp.maximum(old_max, jnp.max(scores, axis=-1))
    powers = jnp.exp(scores - new_max[:, :, None])
    new_total = jnp.sum(powers, axis=-1)
    new_acc = jnp.einsum(
        "hqk,khd->hqd", powers.astype(jnp.bfloat16), value_heads, preferred_element_type=jnp.float32
    )
    enc_attn = (
        (new_acc / new_total[:, :, None])
        .transpose(1, 0, 2)
        .reshape(tok_rows, -1)
        .astype(jnp.bfloat16)
    )
    resid = enc_x.astype(jnp.float32) + jnp.dot(enc_attn, w_eo, preferred_element_type=jnp.float32)
    features = layer_norm(resid).astype(jnp.bfloat16)
    tile_start = doc_tile[0] * TILE_LEN
    x_float = dec_x.astype(jnp.float32)
    normed = (
        x_float * lax.rsqrt(jnp.mean(x_float * x_float, axis=-1, keepdims=True) + 1e-05)
    ).astype(jnp.bfloat16)
    query_cols = jnp.dot(
        lax.all_gather(normed, "seq", axis=0, tiled=True), w_q, preferred_element_type=jnp.float32
    ).astype(jnp.bfloat16)
    query_row = lax.all_to_all(query_cols, "seq", split_axis=0, concat_axis=1, tiled=True)
    zero = jnp.zeros((), jnp.int32)
    filled = cached_count[0]
    local_kv = jnp.dot(features, w_kv, preferred_element_type=jnp.float32).astype(jnp.bfloat16)
    buffer = jnp.zeros((TILE_LEN, w_kv.shape[1]), jnp.bfloat16)
    piece = lax.all_gather(local_kv, "seq", axis=0, tiled=True)
    length = piece.shape[0]
    position = jnp.arange(length, dtype=jnp.int32) - tile_start
    inside = (position >= 0) & (position < buffer.shape[0])
    clipped = jnp.clip(position, 0, buffer.shape[0] - 1)
    tile_kv = buffer.at[clipped].add(jnp.where(inside[:, None], piece, jnp.zeros_like(piece)))
    doc_kv = lax.dynamic_update_slice(cache_kv[0], tile_kv[None], (filled, zero, zero))
    doc_kv = doc_kv.reshape(-1, doc_kv.shape[-1])
    dec_attn = doc_attend(query_row[0], doc_kv, filled)
    output_cols = jnp.dot(
        lax.all_gather(dec_attn, "seq", axis=0, tiled=True), w_o, preferred_element_type=jnp.float32
    ).astype(jnp.bfloat16)
    attn_out = lax.all_to_all(output_cols, "seq", split_axis=0, concat_axis=1, tiled=True)
    return (x_float + attn_out.astype(jnp.float32)).astype(jnp.bfloat16)


def fused_kernel(
    n, enc_ref, x_ref, tile_ref, count_ref, weo_hbm, wkv_hbm, wq_hbm, wo_hbm, cache_hbm, out_ref,
    weo, wkv, wq, wo, cache, load_sem,
    enc_all, enc_send, enc_recv, enc_rows, enc_feat, new_kv,
    norm_own, norm_all, norm_send, norm_recv,
    attn_heads, attn_own, attn_all, attn_send, attn_recv,
    wide, lhs, head_rows,
    q_out, q_in, q_send, q_recv,
    o_out, o_in, o_send, o_recv,
):
    me = lax.axis_index("seq")
    inner = 4
    outer = n // (2 * inner)
    zi, qi, ci = me // (2 * inner), (me // 2) % inner, me % 2

    def at(kz, kq, kc):
        return (zi + kz) % outer * (2 * inner) + (qi + kq) % inner * 2 + (ci + kc) % 2

    loads = [
        pltpu.make_async_copy(src, dst, load_sem.at[i])
        for i, (src, dst) in enumerate(
            ((wq_hbm, wq), (weo_hbm, weo), (wkv_hbm, wkv), (cache_hbm, cache), (wo_hbm, wo))
        )
    ]
    for load in loads:
        load.start()

    barrier = pltpu.get_barrier_semaphore()

    def greet(k, carry):
        pl.semaphore_signal(barrier, inc=1, device_id={"seq": (me + k) % n}, device_id_type=MESH)
        return carry

    lax.fori_loop(1, n, greet, 0)

    x_float = x_ref[...].astype(jnp.float32)
    squares = jnp.sum(jnp.sum(x_float * x_float, axis=1, keepdims=True), axis=0, keepdims=True)
    normed = (x_float * lax.rsqrt(squares / x_float.size + 1e-05)).astype(jnp.bfloat16)
    norm_own[...] = normed
    norm_all[me] = normed
    enc_all[me] = enc_ref[...]
    q_out[...] = jnp.zeros_like(q_out)
    o_out[...] = jnp.zeros_like(o_out)
    pl.semaphore_wait(barrier, n - 1)

    def gather(own, every, send, recv):
        def push(src, slot, sem, device):
            pltpu.make_async_remote_copy(
                src_ref=src, dst_ref=every.at[slot], send_sem=send.at[sem], recv_sem=recv.at[slot],
                device_id={"seq": device}, device_id_type=MESH,
            ).start()

        def take(slot):
            pltpu.make_async_remote_copy(
                src_ref=own, dst_ref=every.at[slot], send_sem=send.at[0], recv_sem=recv.at[slot],
                device_id={"seq": at(0, 0, 1)}, device_id_type=MESH,
            ).wait_recv()

        def first():
            for kz in range(1, outer):
                push(own, me, kz - 1, at(kz, 0, 0))
            for kq in range(1, inner):
                push(own, me, outer - 1 + kq - 1, at(0, kq, 0))
            push(own, me, outer - 1 + inner - 1, at(0, 0, 1))

        def second():
            for kz in range(1, outer):
                slot = at(-kz + outer, 0, 0)
                take(slot)
                base = outer - 1 + inner * kz
                for kq in range(1, inner):
                    push(every.at[slot], slot, base + kq - 1, at(0, kq, 0))
                push(every.at[slot], slot, base + inner - 1, at(0, 0, 1))

        def third():
            base = outer - 1 + inner * outer
            for kz in range(outer):
                for kq in range(1, inner):
                    slot = at(-kz + outer, -kq + inner, 0)
                    take(slot)
                    push(every.at[slot], slot, base + kz * (inner - 1) + kq - 1, at(0, 0, 1))

        def last():
            for kz in range(outer):
                for kq in range(inner):
                    take(at(-kz + outer, -kq + inner, 1))

        def drain():
            def one(k, carry):
                pltpu.make_async_remote_copy(
                    src_ref=own, dst_ref=every.at[0], send_sem=send.at[k], recv_sem=recv.at[0],
                    device_id={"seq": at(0, 0, 1)}, device_id_type=MESH,
                ).wait_send()
                return carry

            lax.fori_loop(0, n - 1, one, 0)

        return first, second, third, last, drain

    def rows_of(ref, index):
        return ref.at[pl.ds(pl.multiple_of(index * 8, 8), 8), :]

    def scatter(values, out, into, send, recv):
        rounded = values.astype(jnp.bfloat16).astype(jnp.float32)
        out[pl.ds(0, n, stride=8), :] = rounded[:, :HD]
        out[pl.ds(1, n, stride=8), :] = rounded[:, HD:]

        def one(k, carry):
            device = (me + k) % n
            pltpu.make_async_remote_copy(
                src_ref=rows_of(out, device), dst_ref=rows_of(into, me),
                send_sem=send.at[k - 1], recv_sem=recv.at[me],
                device_id={"seq": device}, device_id_type=MESH,
            ).start()
            return carry

        lax.fori_loop(1, n, one, 0)
        mine = pl.ds(pl.multiple_of(me * 8, 8), 8)
        into[mine, :] = out[mine, :]

    def collect(out, into, send, recv):
        def one(k, carry):
            source = (me + k) % n
            copy = pltpu.make_async_remote_copy(
                src_ref=rows_of(out, source), dst_ref=rows_of(into, source),
                send_sem=send.at[k - 1], recv_sem=recv.at[source],
                device_id={"seq": source}, device_id_type=MESH,
            )
            copy.wait_recv()
            copy.wait_send()
            return carry

        lax.fori_loop(1, n, one, 0)
        head_rows[pl.ds(0, n, stride=2), :] = into[pl.ds(0, n, stride=8), :]
        head_rows[pl.ds(1, n, stride=2), :] = into[pl.ds(1, n, stride=8), :]

    heads = x_ref.shape[0]

    def project(every, weight):
        wide[...] = every[...].astype(jnp.float32).reshape(n * heads, HD)
        for k in range(heads):
            lhs[:, k * HD:(k + 1) * HD] = wide[pl.ds(k, n, stride=heads), :].astype(jnp.bfloat16)
        return jnp.dot(lhs[...], weight[...], preferred_element_type=jnp.float32)

    norm_first, norm_second, norm_third, norm_last, norm_drain = gather(norm_own, norm_all, norm_send, norm_recv)
    enc_first, enc_second, enc_third, enc_last, enc_drain = gather(enc_ref, enc_all, enc_send, enc_recv)
    norm_first()
    enc_first()
    norm_second()
    norm_third()
    norm_last()
    enc_second()
    loads[0].wait()
    scatter(project(norm_all, wq), q_out, q_in, q_send, q_recv)
    enc_third()
    enc_last()

    tok_rows = enc_ref.shape[0]
    group = 32 // tok_rows

    def unpack(j, carry):
        block = enc_all[pl.ds(j * group, group)].astype(jnp.float32)
        enc_rows[pl.ds(pl.multiple_of(j * 32, 32), 32), :] = block.reshape(32, -1).astype(jnp.bfloat16)
        return carry

    lax.fori_loop(0, n // group, unpack, 0)

    wide_a = EH * EHD

    def own_tile(cols):
        rows = enc_rows[:TILE_LEN, cols].astype(jnp.float32)
        chosen = jnp.broadcast_to(tile_ref[...], rows.shape)
        for t in range(1, enc_rows.shape[0] // TILE_LEN):
            there = enc_rows[t * TILE_LEN:(t + 1) * TILE_LEN, cols].astype(jnp.float32)
            rows = jnp.where(chosen == t, there, rows)
        return rows

    queries = own_tile(slice(0, wide_a)).astype(jnp.bfloat16)
    lane = lax.broadcasted_iota(jnp.int32, (TILE_LEN, wide_a), 1)

    def enc_head(h, acc):
        inside = (lane >= h * EHD) & (lane < (h + 1) * EHD)
        picked = jnp.where(inside, queries, jnp.zeros_like(queries))
        scores = lax.dot_general(
            picked, enc_rows[:, wide_a:2 * wide_a], (((1,), (1,)), ((), ())),
            preferred_element_type=jnp.float32,
        ) * EHD ** (-0.5)
        powers = jnp.exp(scores - jnp.max(scores, axis=-1, keepdims=True))
        weights = (powers / jnp.sum(powers, axis=-1, keepdims=True)).astype(jnp.bfloat16)
        part = jnp.dot(weights, enc_rows[:, 2 * wide_a:3 * wide_a], preferred_element_type=jnp.float32)
        return jnp.where(inside, part, acc)

    enc_attn = lax.fori_loop(0, EH, enc_head, jnp.zeros((TILE_LEN, wide_a), jnp.float32)).astype(jnp.bfloat16)
    loads[1].wait()
    resid = own_tile(slice(3 * wide_a, enc_rows.shape[1])) + jnp.dot(
        enc_attn, weo[...], preferred_element_type=jnp.float32
    )
    enc_feat[...] = layer_norm(resid).astype(jnp.bfloat16)
    loads[2].wait()

    def kv_columns(j, carry):
        cols = pl.ds(pl.multiple_of(j * 256, 256), 256)
        new_kv[:, cols] = jnp.dot(
            enc_feat[...], wkv[:, cols], preferred_element_type=jnp.float32
        ).astype(jnp.bfloat16)
        return carry

    lax.fori_loop(0, new_kv.shape[1] // 256, kv_columns, 0)

    loads[3].wait()
    collect(q_out, q_in, q_send, q_recv)
    slots = cache.shape[0]
    width = new_kv.shape[1] // 2
    kv_heads = width // HD
    each = heads // kv_heads
    token = lax.broadcasted_iota(jnp.int32, (each, slots * TILE_LEN), 1)
    cached = token // TILE_LEN < jnp.broadcast_to(count_ref[...], token.shape)
    flip = (((1,), (1,)), ((), ()))
    for g in range(kv_heads):
        query = head_rows[g * each:(g + 1) * each, :].astype(jnp.bfloat16)
        keys = slice(g * HD, (g + 1) * HD)
        values = slice(width + g * HD, width + (g + 1) * HD)
        old = lax.dot_general(
            query, cache[:, :, keys].reshape(-1, HD), flip, preferred_element_type=jnp.float32
        ) * HD ** (-0.5)
        old = jnp.where(cached, old, -jnp.inf)
        new = lax.dot_general(
            query, new_kv[:, keys], flip, preferred_element_type=jnp.float32
        ) * HD ** (-0.5)
        top = jnp.maximum(jnp.max(old, axis=-1, keepdims=True), jnp.max(new, axis=-1, keepdims=True))
        old = jnp.exp(old - top)
        new = jnp.exp(new - top)
        total = jnp.sum(old, axis=-1, keepdims=True) + jnp.sum(new, axis=-1, keepdims=True)
        attn_heads[g * each:(g + 1) * each, :] = jnp.dot(
            (old / total).astype(jnp.bfloat16), cache[:, :, values].reshape(-1, HD),
            preferred_element_type=jnp.float32,
        ) + jnp.dot(
            (new / total).astype(jnp.bfloat16), new_kv[:, values], preferred_element_type=jnp.float32
        )
    dec_attn = attn_heads[...].astype(jnp.bfloat16)
    attn_own[...] = dec_attn
    attn_all[me] = dec_attn
    attn_first, attn_second, attn_third, attn_last, attn_drain = gather(attn_own, attn_all, attn_send, attn_recv)
    attn_first()
    attn_second()
    attn_third()
    attn_last()
    loads[4].wait()
    scatter(project(attn_all, wo), o_out, o_in, o_send, o_recv)
    norm_drain()
    enc_drain()
    attn_drain()
    collect(o_out, o_in, o_send, o_recv)
    out_ref[...] = (x_ref[...].astype(jnp.float32) + head_rows[...]).astype(jnp.bfloat16)


def fused(n, enc_x, enc_qkv, w_eo, w_kv, dec_x, w_q, w_o, cache_kv, doc_tile, cached_count):
    tok_rows = enc_x.shape[0]
    packed = jnp.concatenate([enc_qkv.reshape(tok_rows, -1), enc_x], axis=1)
    heads = dec_x.shape[1] // HD
    tokens = n * tok_rows
    bf16, f32 = jnp.bfloat16, jnp.float32
    vmem = pl.BlockSpec(memory_space=pltpu.VMEM)
    hbm = pl.BlockSpec(memory_space=pl.ANY)
    dma = pltpu.SemaphoreType.DMA
    piece = [pltpu.VMEM((heads, HD), bf16), pltpu.VMEM((n, heads, HD), bf16), dma((n,)), dma((n,))]
    trade = [pltpu.VMEM((8 * n, HD), f32), pltpu.VMEM((8 * n, HD), f32), dma((n,)), dma((n,))]
    out = pl.pallas_call(
        functools.partial(fused_kernel, n),
        out_shape=jax.ShapeDtypeStruct((heads, HD), bf16),
        in_specs=[vmem, vmem, vmem, vmem, hbm, hbm, hbm, hbm, hbm],
        out_specs=vmem,
        scratch_shapes=[
            pltpu.VMEM(w_eo.shape, bf16),
            pltpu.VMEM(w_kv.shape, bf16),
            pltpu.VMEM(w_q.shape, bf16),
            pltpu.VMEM(w_o.shape, bf16),
            pltpu.VMEM(cache_kv.shape[1:], bf16),
            dma((5,)),
            pltpu.VMEM((n,) + packed.shape, bf16),
            dma((n,)),
            dma((n,)),
            pltpu.VMEM((tokens, packed.shape[1]), bf16),
            pltpu.VMEM((TILE_LEN, enc_x.shape[1]), bf16),
            pltpu.VMEM((TILE_LEN, w_kv.shape[1]), bf16),
            *piece,
            pltpu.VMEM((heads, HD), f32),
            *piece,
            pltpu.VMEM((n * heads, HD), f32),
            pltpu.VMEM((n, heads * HD), bf16),
            pltpu.VMEM((heads, HD), f32),
            *trade,
            *trade,
        ],
        compiler_params=pltpu.CompilerParams(collective_id=0, has_side_effects=True),
    )(packed, dec_x.reshape(heads, HD), doc_tile.reshape(1, 1), cached_count.reshape(1, 1), w_eo, w_kv, w_q, w_o, cache_kv[0])
    return out.reshape(1, -1)


def solution(mesh):
    n = mesh.shape["seq"]
    return jax.shard_map(
        functools.partial(fused, n) if n == 32 else local,
        mesh=mesh,
        in_specs=(
            P(("group", "seq"), None),
            P(("group", "seq"), None, None),
            P(),
            P(),
            P(("group", "seq"), None),
            P(None, "seq"),
            P(None, "seq"),
            P(("group", "seq"), None, None, None),
            P(("group", "seq")),
            P(("group", "seq")),
        ),
        out_specs=P(("group", "seq"), None),
        check_vma=False,
    )
```

```python
import functools

import jax
import jax.numpy as jnp
from jax import lax
from jax.experimental import pallas as pl
from jax.experimental.pallas import tpu as pltpu
from jax.sharding import PartitionSpec as P

EH = 8
EHD = 80
HD = 128
TILE_LEN = 128
MESH = pl.DeviceIdType.MESH


def layer_norm(values):
    center = values - jnp.mean(values, axis=-1, keepdims=True)
    spread = jnp.mean(center * center, axis=-1, keepdims=True)
    return center * lax.rsqrt(spread + 1e-05)


def doc_attend(query_row, doc_kv, filled):
    length = doc_kv.shape[0]
    width = doc_kv.shape[1] // 2
    kv_heads = width // HD
    query_heads = query_row.reshape(kv_heads, -1, HD)
    key_heads = doc_kv[:, :width].reshape(length, kv_heads, HD)
    value_heads = doc_kv[:, width:].reshape(length, kv_heads, HD)
    scores = jnp.einsum(
        "gqd,kgd->gqk", query_heads, key_heads, preferred_element_type=jnp.float32
    ) * HD ** (-0.5)
    inside = jnp.arange(length, dtype=jnp.int32) // TILE_LEN <= filled
    scores = jnp.where(inside[None, None, :], scores, -jnp.inf)
    weights = jax.nn.softmax(scores, axis=-1).astype(jnp.bfloat16)
    result = jnp.einsum("gqk,kgd->gqd", weights, value_heads, preferred_element_type=jnp.float32)
    return result.reshape(1, -1).astype(jnp.bfloat16)


def local(enc_x, enc_qkv, w_eo, w_kv, dec_x, w_q, w_o, cache_kv, doc_tile, cached_count):
    tok_rows = enc_x.shape[0]
    query_heads = enc_qkv[:, 0].reshape(tok_rows, EH, EHD)
    key_piece = lax.all_gather(enc_qkv[:, 1], "seq", axis=0, tiled=True)
    value_piece = lax.all_gather(enc_qkv[:, 2], "seq", axis=0, tiled=True)
    length = key_piece.shape[0]
    key_heads = key_piece.reshape(length, EH, EHD)
    value_heads = value_piece.reshape(length, EH, EHD)
    scores = jnp.einsum(
        "qhd,khd->hqk", query_heads, key_heads, preferred_element_type=jnp.float32
    ) * EHD ** (-0.5)
    old_max = jnp.full((EH, tok_rows), -1e30, jnp.float32)
    new_max = jnp.maximum(old_max, jnp.max(scores, axis=-1))
    powers = jnp.exp(scores - new_max[:, :, None])
    new_total = jnp.sum(powers, axis=-1)
    new_acc = jnp.einsum(
        "hqk,khd->hqd", powers.astype(jnp.bfloat16), value_heads, preferred_element_type=jnp.float32
    )
    enc_attn = (
        (new_acc / new_total[:, :, None])
        .transpose(1, 0, 2)
        .reshape(tok_rows, -1)
        .astype(jnp.bfloat16)
    )
    resid = enc_x.astype(jnp.float32) + jnp.dot(enc_attn, w_eo, preferred_element_type=jnp.float32)
    features = layer_norm(resid).astype(jnp.bfloat16)
    tile_start = doc_tile[0] * TILE_LEN
    x_float = dec_x.astype(jnp.float32)
    normed = (
        x_float * lax.rsqrt(jnp.mean(x_float * x_float, axis=-1, keepdims=True) + 1e-05)
    ).astype(jnp.bfloat16)
    query_cols = jnp.dot(
        lax.all_gather(normed, "seq", axis=0, tiled=True), w_q, preferred_element_type=jnp.float32
    ).astype(jnp.bfloat16)
    query_row = lax.all_to_all(query_cols, "seq", split_axis=0, concat_axis=1, tiled=True)
    zero = jnp.zeros((), jnp.int32)
    filled = cached_count[0]
    local_kv = jnp.dot(features, w_kv, preferred_element_type=jnp.float32).astype(jnp.bfloat16)
    buffer = jnp.zeros((TILE_LEN, w_kv.shape[1]), jnp.bfloat16)
    piece = lax.all_gather(local_kv, "seq", axis=0, tiled=True)
    length = piece.shape[0]
    position = jnp.arange(length, dtype=jnp.int32) - tile_start
    inside = (position >= 0) & (position < buffer.shape[0])
    clipped = jnp.clip(position, 0, buffer.shape[0] - 1)
    tile_kv = buffer.at[clipped].add(jnp.where(inside[:, None], piece, jnp.zeros_like(piece)))
    doc_kv = lax.dynamic_update_slice(cache_kv[0], tile_kv[None], (filled, zero, zero))
    doc_kv = doc_kv.reshape(-1, doc_kv.shape[-1])
    dec_attn = doc_attend(query_row[0], doc_kv, filled)
    output_cols = jnp.dot(
        lax.all_gather(dec_attn, "seq", axis=0, tiled=True), w_o, preferred_element_type=jnp.float32
    ).astype(jnp.bfloat16)
    attn_out = lax.all_to_all(output_cols, "seq", split_axis=0, concat_axis=1, tiled=True)
    return (x_float + attn_out.astype(jnp.float32)).astype(jnp.bfloat16)


def fused_kernel(
    n, qkv_ref, resid_ref, x_ref, tile_ref, count_ref, weo_hbm, wkv_hbm, wq_hbm, wo_hbm, cache_hbm, out_ref,
    weo, wkv, wq, wo, cache, load_sem,
    enc_own, enc_all, enc_send, enc_recv, enc_rows, enc_feat, new_kv,
    x_rows, norm_own, norm_all, norm_send, norm_recv,
    attn_heads, attn_own, attn_all, attn_send, attn_recv,
    wide, lhs, head_rows,
    q_out, q_in, q_send, q_recv,
    o_out, o_in, o_send, o_recv,
):
    me = lax.axis_index("seq")
    inner = 4
    outer = n // (2 * inner)
    zi, qi, ci = me // (2 * inner), (me // 2) % inner, me % 2

    def at(kz, kq, kc):
        return (zi + kz) % outer * (2 * inner) + (qi + kq) % inner * 2 + (ci + kc) % 2

    loads = [
        pltpu.make_async_copy(src, dst, load_sem.at[i])
        for i, (src, dst) in enumerate(
            ((wq_hbm, wq), (weo_hbm, weo), (wkv_hbm, wkv), (cache_hbm, cache), (wo_hbm, wo))
        )
    ]
    for load in loads:
        load.start()

    barrier = pltpu.get_barrier_semaphore()

    partners = [at(kz, 0, 0) for kz in range(1, outer)] + [at(0, kq, 0) for kq in range(1, inner)] + [at(0, 0, 1)]
    for partner in partners:
        pl.semaphore_signal(barrier, inc=1, device_id={"seq": partner}, device_id_type=MESH)

    heads = x_rows.shape[0]
    for k in range(heads):
        x_rows[k:k + 1, :] = x_ref[:, k * HD:(k + 1) * HD].astype(jnp.float32)
    x_float = x_rows[...]
    squares = jnp.sum(jnp.sum(x_float * x_float, axis=1, keepdims=True), axis=0, keepdims=True)
    normed = (x_float * lax.rsqrt(squares / x_float.size + 1e-05)).astype(jnp.bfloat16)
    norm_own[...] = normed
    norm_all[me] = normed
    wide_a = EH * EHD
    for j in range(3):
        enc_own[:, j * wide_a:(j + 1) * wide_a] = qkv_ref[j]
    enc_own[:, 3 * wide_a:] = resid_ref[...]
    enc_all[me] = enc_own[...]
    pl.semaphore_wait(barrier, len(partners))

    def gather(own, every, send, recv):
        def push(src, slot, sem, device):
            pltpu.make_async_remote_copy(
                src_ref=src, dst_ref=every.at[slot], send_sem=send.at[sem], recv_sem=recv.at[slot],
                device_id={"seq": device}, device_id_type=MESH,
            ).start()

        def take(slot):
            pltpu.make_async_remote_copy(
                src_ref=own, dst_ref=every.at[slot], send_sem=send.at[0], recv_sem=recv.at[slot],
                device_id={"seq": at(0, 0, 1)}, device_id_type=MESH,
            ).wait_recv()

        def first():
            for kz in range(1, outer):
                push(own, me, kz - 1, at(kz, 0, 0))
            for kq in range(1, inner):
                push(own, me, outer - 1 + kq - 1, at(0, kq, 0))
            push(own, me, outer - 1 + inner - 1, at(0, 0, 1))

        def second():
            for kz in range(1, outer):
                slot = at(-kz + outer, 0, 0)
                take(slot)
                base = outer - 1 + inner * kz
                for kq in range(1, inner):
                    push(every.at[slot], slot, base + kq - 1, at(0, kq, 0))
                push(every.at[slot], slot, base + inner - 1, at(0, 0, 1))

        def third():
            base = outer - 1 + inner * outer
            for kz in range(outer):
                for kq in range(1, inner):
                    slot = at(-kz + outer, -kq + inner, 0)
                    take(slot)
                    push(every.at[slot], slot, base + kz * (inner - 1) + kq - 1, at(0, 0, 1))

        def last():
            for kz in range(outer):
                for kq in range(inner):
                    take(at(-kz + outer, -kq + inner, 1))

        def drain():
            def one(k, carry):
                pltpu.make_async_remote_copy(
                    src_ref=own, dst_ref=every.at[0], send_sem=send.at[k], recv_sem=recv.at[0],
                    device_id={"seq": at(0, 0, 1)}, device_id_type=MESH,
                ).wait_send()
                return carry

            lax.fori_loop(0, n - 1, one, 0)

        return first, second, third, last, drain

    def scatter(values, out, into, send, recv):
        rounded = values.astype(jnp.bfloat16).astype(jnp.float32)
        for d in range(n):
            for half in range(2):
                out[d, half:half + 1, :] = rounded[d:d + 1, half * HD:(half + 1) * HD]

        def one(k, carry):
            device = (me + k) % n
            pltpu.make_async_remote_copy(
                src_ref=out.at[device], dst_ref=into.at[me],
                send_sem=send.at[k - 1], recv_sem=recv.at[me],
                device_id={"seq": device}, device_id_type=MESH,
            ).start()
            return carry

        lax.fori_loop(1, n, one, 0)
        into[me] = out[me]

    def collect(out, into, send, recv):
        def one(k, carry):
            source = (me + k) % n
            copy = pltpu.make_async_remote_copy(
                src_ref=out.at[source], dst_ref=into.at[source],
                send_sem=send.at[k - 1], recv_sem=recv.at[source],
                device_id={"seq": source}, device_id_type=MESH,
            )
            copy.wait_recv()
            copy.wait_send()
            return carry

        lax.fori_loop(1, n, one, 0)
        for d in range(n):
            head_rows[2 * d:2 * d + 2, :] = into[d]

    def project(every, weight):
        wide[...] = every[...].astype(jnp.float32).reshape(n * heads, HD)
        for k in range(heads):
            lhs[:, k * HD:(k + 1) * HD] = wide[pl.ds(k, n, stride=heads), :].astype(jnp.bfloat16)
        return jnp.dot(lhs[...], weight[...], preferred_element_type=jnp.float32)

    norm_first, norm_second, norm_third, norm_last, norm_drain = gather(norm_own, norm_all, norm_send, norm_recv)
    enc_first, enc_second, enc_third, enc_last, enc_drain = gather(enc_own, enc_all, enc_send, enc_recv)
    norm_first()
    enc_first()
    norm_second()
    norm_third()
    norm_last()
    enc_second()
    loads[0].wait()
    scatter(project(norm_all, wq), q_out, q_in, q_send, q_recv)
    enc_third()
    enc_last()

    tok_rows = enc_own.shape[0]
    group = 32 // tok_rows

    def unpack(j, carry):
        block = enc_all[pl.ds(j * group, group), :, wide_a:3 * wide_a].astype(jnp.float32)
        enc_rows[pl.ds(pl.multiple_of(j * 32, 32), 32), :] = block.reshape(32, -1).astype(jnp.bfloat16)
        return carry

    lax.fori_loop(0, n // group, unpack, 0)
    each_tile = TILE_LEN // tok_rows

    def own_tile(cols):
        rows = None
        for t in range(n // each_tile):
            there = enc_all[t * each_tile:(t + 1) * each_tile, :, cols].astype(jnp.float32)
            there = there.reshape(TILE_LEN, -1)
            if rows is None:
                rows, chosen = there, jnp.broadcast_to(tile_ref[...], there.shape)
            else:
                rows = jnp.where(chosen == t, there, rows)
        return rows

    queries = own_tile(slice(0, wide_a)).astype(jnp.bfloat16)
    columns = [None] * (wide_a // HD)
    for h in range(EH):
        low, high = h * EHD // HD, (h * EHD + EHD - 1) // HD + 1
        span = slice(low * HD, high * HD)
        lane = lax.broadcasted_iota(jnp.int32, (TILE_LEN, (high - low) * HD), 1) + low * HD
        inside = (lane >= h * EHD) & (lane < (h + 1) * EHD)
        picked = jnp.where(inside, queries[:, span], jnp.zeros_like(queries[:, span]))
        scores = lax.dot_general(
            picked, enc_rows[:, span], (((1,), (1,)), ((), ())), preferred_element_type=jnp.float32
        ) * EHD ** (-0.5)
        powers = jnp.exp(scores - jnp.max(scores, axis=-1, keepdims=True))
        weights = (powers / jnp.sum(powers, axis=-1, keepdims=True)).astype(jnp.bfloat16)
        part = jnp.dot(
            weights, enc_rows[:, wide_a + low * HD:wide_a + high * HD], preferred_element_type=jnp.float32
        )
        for b in range(low, high):
            here = slice((b - low) * HD, (b - low + 1) * HD)
            columns[b] = part[:, here] if columns[b] is None else jnp.where(inside[:, here], part[:, here], columns[b])
    enc_attn = jnp.concatenate(columns, axis=1).astype(jnp.bfloat16)
    loads[1].wait()
    resid = own_tile(slice(3 * wide_a, enc_own.shape[1])) + jnp.dot(
        enc_attn, weo[...], preferred_element_type=jnp.float32
    )
    enc_feat[...] = layer_norm(resid).astype(jnp.bfloat16)
    loads[2].wait()

    def kv_columns(j, carry):
        cols = pl.ds(pl.multiple_of(j * 512, 512), 512)
        new_kv[:, cols] = jnp.dot(
            enc_feat[...], wkv[:, cols], preferred_element_type=jnp.float32
        ).astype(jnp.bfloat16)
        return carry

    lax.fori_loop(0, new_kv.shape[1] // 512, kv_columns, 0)

    loads[3].wait()
    collect(q_out, q_in, q_send, q_recv)
    slots = cache.shape[0]
    width = new_kv.shape[1] // 2
    kv_heads = width // HD
    each = heads // kv_heads
    token = lax.broadcasted_iota(jnp.int32, (each, slots * TILE_LEN), 1)
    cached = token // TILE_LEN < jnp.broadcast_to(count_ref[...], token.shape)
    flip = (((1,), (1,)), ((), ()))
    for g in range(kv_heads):
        query = head_rows[g * each:(g + 1) * each, :].astype(jnp.bfloat16)
        keys = slice(g * HD, (g + 1) * HD)
        values = slice(width + g * HD, width + (g + 1) * HD)
        old = lax.dot_general(
            query, cache[:, :, keys].reshape(-1, HD), flip, preferred_element_type=jnp.float32
        ) * HD ** (-0.5)
        old = jnp.where(cached, old, -jnp.inf)
        new = lax.dot_general(
            query, new_kv[:, keys], flip, preferred_element_type=jnp.float32
        ) * HD ** (-0.5)
        top = jnp.maximum(jnp.max(old, axis=-1, keepdims=True), jnp.max(new, axis=-1, keepdims=True))
        old = jnp.exp(old - top)
        new = jnp.exp(new - top)
        total = jnp.sum(old, axis=-1, keepdims=True) + jnp.sum(new, axis=-1, keepdims=True)
        attn_heads[g * each:(g + 1) * each, :] = jnp.dot(
            (old / total).astype(jnp.bfloat16), cache[:, :, values].reshape(-1, HD),
            preferred_element_type=jnp.float32,
        ) + jnp.dot(
            (new / total).astype(jnp.bfloat16), new_kv[:, values], preferred_element_type=jnp.float32
        )
    dec_attn = attn_heads[...].astype(jnp.bfloat16)
    attn_own[...] = dec_attn
    attn_all[me] = dec_attn
    attn_first, attn_second, attn_third, attn_last, attn_drain = gather(attn_own, attn_all, attn_send, attn_recv)
    attn_first()
    attn_second()
    attn_third()
    attn_last()
    loads[4].wait()
    scatter(project(attn_all, wo), o_out, o_in, o_send, o_recv)
    norm_drain()
    enc_drain()
    attn_drain()
    collect(o_out, o_in, o_send, o_recv)
    out_ref[...] = (x_rows[...] + head_rows[...]).astype(jnp.bfloat16)


def fused(n, enc_x, enc_qkv, w_eo, w_kv, dec_x, w_q, w_o, cache_kv, doc_tile, cached_count):
    tok_rows = enc_x.shape[0]
    packed = (tok_rows, enc_qkv.shape[1] * enc_qkv.shape[2] + enc_x.shape[1])
    heads = dec_x.shape[1] // HD
    tokens = n * tok_rows
    bf16, f32 = jnp.bfloat16, jnp.float32
    vmem = pl.BlockSpec(memory_space=pltpu.VMEM)
    hbm = pl.BlockSpec(memory_space=pl.ANY)
    dma = pltpu.SemaphoreType.DMA
    piece = [pltpu.VMEM((heads, HD), bf16), pltpu.VMEM((n, heads, HD), bf16), dma((n,)), dma((n,))]
    trade = [pltpu.VMEM((n, 2, HD), f32), pltpu.VMEM((n, 2, HD), f32), dma((n,)), dma((n,))]
    out = pl.pallas_call(
        functools.partial(fused_kernel, n),
        out_shape=jax.ShapeDtypeStruct((heads, HD), bf16),
        in_specs=[vmem, vmem, vmem, vmem, vmem, hbm, hbm, hbm, hbm, hbm],
        out_specs=vmem,
        scratch_shapes=[
            pltpu.VMEM(w_eo.shape, bf16),
            pltpu.VMEM(w_kv.shape, bf16),
            pltpu.VMEM(w_q.shape, bf16),
            pltpu.VMEM(w_o.shape, bf16),
            pltpu.VMEM(cache_kv.shape[1:], bf16),
            dma((5,)),
            pltpu.VMEM(packed, bf16),
            pltpu.VMEM((n,) + packed, bf16),
            dma((n,)),
            dma((n,)),
            pltpu.VMEM((tokens, 2 * enc_qkv.shape[2]), bf16),
            pltpu.VMEM((TILE_LEN, enc_x.shape[1]), bf16),
            pltpu.VMEM((TILE_LEN, w_kv.shape[1]), bf16),
            pltpu.VMEM((heads, HD), f32),
            *piece,
            pltpu.VMEM((heads, HD), f32),
            *piece,
            pltpu.VMEM((n * heads, HD), f32),
            pltpu.VMEM((n, heads * HD), bf16),
            pltpu.VMEM((heads, HD), f32),
            *trade,
            *trade,
        ],
        compiler_params=pltpu.CompilerParams(collective_id=0, has_side_effects=True),
    )(enc_qkv.transpose(1, 0, 2), enc_x, dec_x, doc_tile.reshape(1, 1), cached_count.reshape(1, 1), w_eo, w_kv, w_q, w_o, cache_kv[0])
    return out.reshape(1, -1)


def solution(mesh):
    n = mesh.shape["seq"]
    return jax.shard_map(
        functools.partial(fused, n) if n == 32 else local,
        mesh=mesh,
        in_specs=(
            P(("group", "seq"), None),
            P(("group", "seq"), None, None),
            P(),
            P(),
            P(("group", "seq"), None),
            P(None, "seq"),
            P(None, "seq"),
            P(("group", "seq"), None, None, None),
            P(("group", "seq")),
            P(("group", "seq")),
        ),
        out_specs=P(("group", "seq"), None),
        check_vma=False,
    )
```

```python
import functools

import jax
import jax.numpy as jnp
from jax import lax
from jax.experimental import pallas as pl
from jax.experimental.pallas import tpu as pltpu
from jax.sharding import PartitionSpec as P

EH = 8
EHD = 80
HD = 128
TILE_LEN = 128
MESH = pl.DeviceIdType.MESH


def layer_norm(values):
    center = values - jnp.mean(values, axis=-1, keepdims=True)
    spread = jnp.mean(center * center, axis=-1, keepdims=True)
    return center * lax.rsqrt(spread + 1e-05)


def doc_attend(query_row, doc_kv, filled):
    length = doc_kv.shape[0]
    width = doc_kv.shape[1] // 2
    kv_heads = width // HD
    query_heads = query_row.reshape(kv_heads, -1, HD)
    key_heads = doc_kv[:, :width].reshape(length, kv_heads, HD)
    value_heads = doc_kv[:, width:].reshape(length, kv_heads, HD)
    scores = jnp.einsum(
        "gqd,kgd->gqk", query_heads, key_heads, preferred_element_type=jnp.float32
    ) * HD ** (-0.5)
    inside = jnp.arange(length, dtype=jnp.int32) // TILE_LEN <= filled
    scores = jnp.where(inside[None, None, :], scores, -jnp.inf)
    weights = jax.nn.softmax(scores, axis=-1).astype(jnp.bfloat16)
    result = jnp.einsum("gqk,kgd->gqd", weights, value_heads, preferred_element_type=jnp.float32)
    return result.reshape(1, -1).astype(jnp.bfloat16)


def local(enc_x, enc_qkv, w_eo, w_kv, dec_x, w_q, w_o, cache_kv, doc_tile, cached_count):
    tok_rows = enc_x.shape[0]
    query_heads = enc_qkv[:, 0].reshape(tok_rows, EH, EHD)
    key_piece = lax.all_gather(enc_qkv[:, 1], "seq", axis=0, tiled=True)
    value_piece = lax.all_gather(enc_qkv[:, 2], "seq", axis=0, tiled=True)
    length = key_piece.shape[0]
    key_heads = key_piece.reshape(length, EH, EHD)
    value_heads = value_piece.reshape(length, EH, EHD)
    scores = jnp.einsum(
        "qhd,khd->hqk", query_heads, key_heads, preferred_element_type=jnp.float32
    ) * EHD ** (-0.5)
    old_max = jnp.full((EH, tok_rows), -1e30, jnp.float32)
    new_max = jnp.maximum(old_max, jnp.max(scores, axis=-1))
    powers = jnp.exp(scores - new_max[:, :, None])
    new_total = jnp.sum(powers, axis=-1)
    new_acc = jnp.einsum(
        "hqk,khd->hqd", powers.astype(jnp.bfloat16), value_heads, preferred_element_type=jnp.float32
    )
    enc_attn = (
        (new_acc / new_total[:, :, None])
        .transpose(1, 0, 2)
        .reshape(tok_rows, -1)
        .astype(jnp.bfloat16)
    )
    resid = enc_x.astype(jnp.float32) + jnp.dot(enc_attn, w_eo, preferred_element_type=jnp.float32)
    features = layer_norm(resid).astype(jnp.bfloat16)
    tile_start = doc_tile[0] * TILE_LEN
    x_float = dec_x.astype(jnp.float32)
    normed = (
        x_float * lax.rsqrt(jnp.mean(x_float * x_float, axis=-1, keepdims=True) + 1e-05)
    ).astype(jnp.bfloat16)
    query_cols = jnp.dot(
        lax.all_gather(normed, "seq", axis=0, tiled=True), w_q, preferred_element_type=jnp.float32
    ).astype(jnp.bfloat16)
    query_row = lax.all_to_all(query_cols, "seq", split_axis=0, concat_axis=1, tiled=True)
    zero = jnp.zeros((), jnp.int32)
    filled = cached_count[0]
    local_kv = jnp.dot(features, w_kv, preferred_element_type=jnp.float32).astype(jnp.bfloat16)
    buffer = jnp.zeros((TILE_LEN, w_kv.shape[1]), jnp.bfloat16)
    piece = lax.all_gather(local_kv, "seq", axis=0, tiled=True)
    length = piece.shape[0]
    position = jnp.arange(length, dtype=jnp.int32) - tile_start
    inside = (position >= 0) & (position < buffer.shape[0])
    clipped = jnp.clip(position, 0, buffer.shape[0] - 1)
    tile_kv = buffer.at[clipped].add(jnp.where(inside[:, None], piece, jnp.zeros_like(piece)))
    doc_kv = lax.dynamic_update_slice(cache_kv[0], tile_kv[None], (filled, zero, zero))
    doc_kv = doc_kv.reshape(-1, doc_kv.shape[-1])
    dec_attn = doc_attend(query_row[0], doc_kv, filled)
    output_cols = jnp.dot(
        lax.all_gather(dec_attn, "seq", axis=0, tiled=True), w_o, preferred_element_type=jnp.float32
    ).astype(jnp.bfloat16)
    attn_out = lax.all_to_all(output_cols, "seq", split_axis=0, concat_axis=1, tiled=True)
    return (x_float + attn_out.astype(jnp.float32)).astype(jnp.bfloat16)


def fused_kernel(
    n, qkv_ref, resid_ref, x_ref, tile_ref, count_ref, weo_hbm, wkv_hbm, wq_hbm, wo_hbm, cache_hbm, out_ref,
    weo, wkv, wq, wo, cache, load_sem,
    enc_own, enc_all, enc_send, enc_recv, enc_rows, enc_feat, new_kv,
    x_rows, norm_own, norm_all, norm_send, norm_recv,
    attn_heads, attn_own, attn_all, attn_send, attn_recv,
    wide, lhs, head_rows, old_scores,
    q_out, q_in, q_send, q_recv,
    o_out, o_in, o_send, o_recv,
):
    me = lax.axis_index("seq")
    inner = 4
    outer = n // (2 * inner)
    zi, qi, ci = me // (2 * inner), (me // 2) % inner, me % 2

    def at(kz, kq, kc):
        return (zi + kz) % outer * (2 * inner) + (qi + kq) % inner * 2 + (ci + kc) % 2

    loads = [
        pltpu.make_async_copy(src, dst, load_sem.at[i])
        for i, (src, dst) in enumerate(
            ((wq_hbm, wq), (weo_hbm, weo), (wkv_hbm, wkv), (cache_hbm, cache), (wo_hbm, wo))
        )
    ]
    for load in loads:
        load.start()

    barrier = pltpu.get_barrier_semaphore()

    partners = [at(kz, 0, 0) for kz in range(1, outer)] + [at(0, kq, 0) for kq in range(1, inner)] + [at(0, 0, 1)]
    for partner in partners:
        pl.semaphore_signal(barrier, inc=1, device_id={"seq": partner}, device_id_type=MESH)

    heads = x_rows.shape[0]
    for k in range(heads):
        x_rows[k:k + 1, :] = x_ref[:, k * HD:(k + 1) * HD].astype(jnp.float32)
    x_float = x_rows[...]
    squares = jnp.sum(jnp.sum(x_float * x_float, axis=1, keepdims=True), axis=0, keepdims=True)
    normed = (x_float * lax.rsqrt(squares / x_float.size + 1e-05)).astype(jnp.bfloat16)
    norm_own[...] = normed
    norm_all[me] = normed
    wide_a = EH * EHD
    for j in range(3):
        enc_own[:, j * wide_a:(j + 1) * wide_a] = qkv_ref[j]
    enc_own[:, 3 * wide_a:] = resid_ref[...]
    enc_all[me] = enc_own[...]
    pl.semaphore_wait(barrier, len(partners))

    flip_x = qi + 1 - 2 * (qi % 2)
    flip_y = (qi + 2) % inner
    flip_both = (flip_x + 2) % inner

    def place(kz, plane, core):
        return (zi + kz + outer) % outer * (2 * inner) + plane * 2 + core

    def gather(own, every, send, recv, relay):
        sent = [0]

        def push(src, slot, device):
            pltpu.make_async_remote_copy(
                src_ref=src, dst_ref=every.at[slot], send_sem=send.at[sent[0]], recv_sem=recv.at[slot],
                device_id={"seq": device}, device_id_type=MESH,
            ).start()
            sent[0] += 1

        def take(slot):
            pltpu.make_async_remote_copy(
                src_ref=own, dst_ref=every.at[slot], send_sem=send.at[0], recv_sem=recv.at[slot],
                device_id={"seq": place(0, qi, 1 - ci)}, device_id_type=MESH,
            ).wait_recv()

        def spread(src, slot):
            for plane in (flip_x, flip_y) if relay else (flip_both, flip_x, flip_y):
                push(src, slot, place(0, plane, ci))
            push(src, slot, place(0, qi, 1 - ci))

        def first():
            for kz in range(1, outer):
                push(own, me, place(kz, qi, ci))
            spread(own, me)

        def second():
            for kz in range(1, outer):
                slot = place(-kz, qi, ci)
                take(slot)
                spread(every.at[slot], slot)

        def third():
            for kz in range(outer):
                for odd, (plane, onward) in enumerate(((flip_x, flip_y), (flip_y, flip_x))):
                    slot = place(-kz, plane, ci)
                    take(slot)
                    if relay and kz % 2 == odd:
                        push(every.at[slot], slot, place(0, onward, ci))
                    push(every.at[slot], slot, place(0, qi, 1 - ci))

        def fourth():
            for kz in range(outer):
                slot = place(-kz, flip_both, ci)
                take(slot)
                push(every.at[slot], slot, place(0, qi, 1 - ci))

        def last():
            for plane in (qi, flip_x, flip_y, flip_both):
                for kz in range(outer):
                    take(place(-kz, plane, 1 - ci))

        def drain():
            def one(k, carry):
                pltpu.make_async_remote_copy(
                    src_ref=own, dst_ref=every.at[0], send_sem=send.at[k], recv_sem=recv.at[0],
                    device_id={"seq": place(0, qi, 1 - ci)}, device_id_type=MESH,
                ).wait_send()
                return carry

            lax.fori_loop(0, n - 1, one, 0)

        return first, second, third, fourth, last, drain

    def scatter(values, out, into, send, recv):
        rounded = values.astype(jnp.bfloat16).astype(jnp.float32)
        for d in range(n):
            for half in range(2):
                out[d, half:half + 1, :] = rounded[d:d + 1, half * HD:(half + 1) * HD]

        def one(k, carry):
            device = (me + k) % n
            pltpu.make_async_remote_copy(
                src_ref=out.at[device], dst_ref=into.at[me],
                send_sem=send.at[k - 1], recv_sem=recv.at[me],
                device_id={"seq": device}, device_id_type=MESH,
            ).start()
            return carry

        lax.fori_loop(1, n, one, 0)
        into[me] = out[me]

    def collect(out, into, send, recv):
        def one(k, carry):
            source = (me + k) % n
            copy = pltpu.make_async_remote_copy(
                src_ref=out.at[source], dst_ref=into.at[source],
                send_sem=send.at[k - 1], recv_sem=recv.at[source],
                device_id={"seq": source}, device_id_type=MESH,
            )
            copy.wait_recv()
            copy.wait_send()
            return carry

        lax.fori_loop(1, n, one, 0)
        for d in range(n):
            head_rows[2 * d:2 * d + 2, :] = into[d]

    def project(every, weight):
        wide[...] = every[...].astype(jnp.float32).reshape(n * heads, HD)
        for k in range(heads):
            lhs[:, k * HD:(k + 1) * HD] = wide[pl.ds(k, n, stride=heads), :].astype(jnp.bfloat16)
        return jnp.dot(lhs[...], weight[...], preferred_element_type=jnp.float32)

    norm_first, norm_second, norm_third, norm_fourth, norm_last, norm_drain = gather(
        norm_own, norm_all, norm_send, norm_recv, False
    )
    enc_first, enc_second, enc_third, enc_fourth, enc_last, enc_drain = gather(
        enc_own, enc_all, enc_send, enc_recv, True
    )
    norm_first()
    enc_first()
    norm_second()
    enc_second()
    norm_third()
    norm_fourth()
    norm_last()
    loads[0].wait()
    scatter(project(norm_all, wq), q_out, q_in, q_send, q_recv)
    enc_third()
    enc_fourth()
    loads[3].wait()
    collect(q_out, q_in, q_send, q_recv)
    width = new_kv.shape[1] // 2
    kv_heads = width // HD
    each = heads // kv_heads
    flip = (((1,), (1,)), ((), ()))
    for g in range(kv_heads):
        old_scores[g * each:(g + 1) * each, :] = lax.dot_general(
            head_rows[g * each:(g + 1) * each, :].astype(jnp.bfloat16),
            cache[:, :, g * HD:(g + 1) * HD].reshape(-1, HD), flip, preferred_element_type=jnp.float32,
        ) * HD ** (-0.5)
    enc_last()

    tok_rows = enc_own.shape[0]
    group = 32 // tok_rows

    def unpack(j, carry):
        block = enc_all[pl.ds(j * group, group), :, wide_a:3 * wide_a].astype(jnp.float32)
        enc_rows[pl.ds(pl.multiple_of(j * 32, 32), 32), :] = block.reshape(32, -1).astype(jnp.bfloat16)
        return carry

    lax.fori_loop(0, n // group, unpack, 0)
    each_tile = TILE_LEN // tok_rows

    def own_tile(cols):
        rows = None
        for t in range(n // each_tile):
            there = enc_all[t * each_tile:(t + 1) * each_tile, :, cols].astype(jnp.float32)
            there = there.reshape(TILE_LEN, -1)
            if rows is None:
                rows, chosen = there, jnp.broadcast_to(tile_ref[...], there.shape)
            else:
                rows = jnp.where(chosen == t, there, rows)
        return rows

    queries = own_tile(slice(0, wide_a)).astype(jnp.bfloat16)
    columns = [None] * (wide_a // HD)
    for h in range(EH):
        low, high = h * EHD // HD, (h * EHD + EHD - 1) // HD + 1
        span = slice(low * HD, high * HD)
        lane = lax.broadcasted_iota(jnp.int32, (TILE_LEN, (high - low) * HD), 1) + low * HD
        inside = (lane >= h * EHD) & (lane < (h + 1) * EHD)
        picked = jnp.where(inside, queries[:, span], jnp.zeros_like(queries[:, span]))
        scores = lax.dot_general(
            picked, enc_rows[:, span], (((1,), (1,)), ((), ())), preferred_element_type=jnp.float32
        ) * EHD ** (-0.5)
        powers = jnp.exp(scores - jnp.max(scores, axis=-1, keepdims=True))
        weights = (powers / jnp.sum(powers, axis=-1, keepdims=True)).astype(jnp.bfloat16)
        part = jnp.dot(
            weights, enc_rows[:, wide_a + low * HD:wide_a + high * HD], preferred_element_type=jnp.float32
        )
        for b in range(low, high):
            here = slice((b - low) * HD, (b - low + 1) * HD)
            columns[b] = part[:, here] if columns[b] is None else jnp.where(inside[:, here], part[:, here], columns[b])
    enc_attn = jnp.concatenate(columns, axis=1).astype(jnp.bfloat16)
    loads[1].wait()
    resid = own_tile(slice(3 * wide_a, enc_own.shape[1])) + jnp.dot(
        enc_attn, weo[...], preferred_element_type=jnp.float32
    )
    enc_feat[...] = layer_norm(resid).astype(jnp.bfloat16)
    loads[2].wait()

    def kv_columns(j, carry):
        cols = pl.ds(pl.multiple_of(j * 512, 512), 512)
        new_kv[:, cols] = jnp.dot(
            enc_feat[...], wkv[:, cols], preferred_element_type=jnp.float32
        ).astype(jnp.bfloat16)
        return carry

    lax.fori_loop(0, new_kv.shape[1] // 512, kv_columns, 0)

    slots = cache.shape[0]
    token = lax.broadcasted_iota(jnp.int32, (each, slots * TILE_LEN), 1)
    cached = token // TILE_LEN < jnp.broadcast_to(count_ref[...], token.shape)
    for g in range(kv_heads):
        query = head_rows[g * each:(g + 1) * each, :].astype(jnp.bfloat16)
        keys = slice(g * HD, (g + 1) * HD)
        values = slice(width + g * HD, width + (g + 1) * HD)
        old = jnp.where(cached, old_scores[g * each:(g + 1) * each, :], -jnp.inf)
        new = lax.dot_general(
            query, new_kv[:, keys], flip, preferred_element_type=jnp.float32
        ) * HD ** (-0.5)
        top = jnp.maximum(jnp.max(old, axis=-1, keepdims=True), jnp.max(new, axis=-1, keepdims=True))
        old = jnp.exp(old - top)
        new = jnp.exp(new - top)
        total = jnp.sum(old, axis=-1, keepdims=True) + jnp.sum(new, axis=-1, keepdims=True)
        attn_heads[g * each:(g + 1) * each, :] = jnp.dot(
            (old / total).astype(jnp.bfloat16), cache[:, :, values].reshape(-1, HD),
            preferred_element_type=jnp.float32,
        ) + jnp.dot(
            (new / total).astype(jnp.bfloat16), new_kv[:, values], preferred_element_type=jnp.float32
        )
    dec_attn = attn_heads[...].astype(jnp.bfloat16)
    attn_own[...] = dec_attn
    attn_all[me] = dec_attn
    attn_first, attn_second, attn_third, attn_fourth, attn_last, attn_drain = gather(
        attn_own, attn_all, attn_send, attn_recv, False
    )
    attn_first()
    attn_second()
    attn_third()
    attn_fourth()
    attn_last()
    loads[4].wait()
    scatter(project(attn_all, wo), o_out, o_in, o_send, o_recv)
    norm_drain()
    enc_drain()
    attn_drain()
    collect(o_out, o_in, o_send, o_recv)
    out_ref[...] = (x_rows[...] + head_rows[...]).astype(jnp.bfloat16)


def fused(n, enc_x, enc_qkv, w_eo, w_kv, dec_x, w_q, w_o, cache_kv, doc_tile, cached_count):
    tok_rows = enc_x.shape[0]
    packed = (tok_rows, enc_qkv.shape[1] * enc_qkv.shape[2] + enc_x.shape[1])
    heads = dec_x.shape[1] // HD
    tokens = n * tok_rows
    bf16, f32 = jnp.bfloat16, jnp.float32
    vmem = pl.BlockSpec(memory_space=pltpu.VMEM)
    hbm = pl.BlockSpec(memory_space=pl.ANY)
    dma = pltpu.SemaphoreType.DMA
    piece = [pltpu.VMEM((heads, HD), bf16), pltpu.VMEM((n, heads, HD), bf16), dma((n,)), dma((n,))]
    trade = [pltpu.VMEM((n, 2, HD), f32), pltpu.VMEM((n, 2, HD), f32), dma((n,)), dma((n,))]
    out = pl.pallas_call(
        functools.partial(fused_kernel, n),
        out_shape=jax.ShapeDtypeStruct((heads, HD), bf16),
        in_specs=[vmem, vmem, vmem, vmem, vmem, hbm, hbm, hbm, hbm, hbm],
        out_specs=vmem,
        scratch_shapes=[
            pltpu.VMEM(w_eo.shape, bf16),
            pltpu.VMEM(w_kv.shape, bf16),
            pltpu.VMEM(w_q.shape, bf16),
            pltpu.VMEM(w_o.shape, bf16),
            pltpu.VMEM(cache_kv.shape[1:], bf16),
            dma((5,)),
            pltpu.VMEM(packed, bf16),
            pltpu.VMEM((n,) + packed, bf16),
            dma((n,)),
            dma((n,)),
            pltpu.VMEM((tokens, 2 * enc_qkv.shape[2]), bf16),
            pltpu.VMEM((TILE_LEN, enc_x.shape[1]), bf16),
            pltpu.VMEM((TILE_LEN, w_kv.shape[1]), bf16),
            pltpu.VMEM((heads, HD), f32),
            *piece,
            pltpu.VMEM((heads, HD), f32),
            *piece,
            pltpu.VMEM((n * heads, HD), f32),
            pltpu.VMEM((n, heads * HD), bf16),
            pltpu.VMEM((heads, HD), f32),
            pltpu.VMEM((heads, cache_kv.shape[1] * TILE_LEN), f32),
            *trade,
            *trade,
        ],
        compiler_params=pltpu.CompilerParams(collective_id=0, has_side_effects=True),
    )(enc_qkv.transpose(1, 0, 2), enc_x, dec_x, doc_tile.reshape(1, 1), cached_count.reshape(1, 1), w_eo, w_kv, w_q, w_o, cache_kv[0])
    return out.reshape(1, -1)


def solution(mesh):
    n = mesh.shape["seq"]
    return jax.shard_map(
        functools.partial(fused, n) if n == 32 else local,
        mesh=mesh,
        in_specs=(
            P(("group", "seq"), None),
            P(("group", "seq"), None, None),
            P(),
            P(),
            P(("group", "seq"), None),
            P(None, "seq"),
            P(None, "seq"),
            P(("group", "seq"), None, None, None),
            P(("group", "seq")),
            P(("group", "seq")),
        ),
        out_specs=P(("group", "seq"), None),
        check_vma=False,
    )
```
